32 devices in a mesh: groups: 2 (over y), feat: 4 (over z), dp: 2 (over x), section: 2 (over core).
Axes of the slice: x: 2, y: 2, z: 4, core: 2. Of those that a mesh axis runs over, the one named last changes fastest.
Arguments:
- residuals: bfloat16 [2, 3072, 8192], P('section', ('groups', 'dp'), 'feat'), parts along dimension 1, may hold values from -6 to 6
- final_resid: bfloat16 [3072, 8192], P(('groups', 'dp', 'section'), 'feat'), parts along dimension 0, may hold values from -6 to 6
- final_order: int32 [3072], P(('groups', 'dp')), parts along dimension 0, may hold values from 0 to 767, as said below
- translator: bfloat16 [2, 8192, 8192], P('section', 'dp', 'feat'), may hold values from -0.0625 to 0.0625
- bias: float32 [2, 8192], P('section', 'feat'), may hold values from -5 to 5
Outputs:
- grad_weight: bfloat16 [4, 8192, 8192], P(('groups', 'section'), 'dp', 'feat'), parts along dimension 0
- grad_bias: float32 [4, 8192], P(('groups', 'section'), 'feat'), parts along dimension 0
The draws below stay inside these ranges and needn't reach their ends.
There are 2 independent parts, one for each index of `groups`. The reference program is written for one: setup_inputs(seed, part) draws one part's arguments, and reference() takes and returns one part's arrays. A program takes and returns all parts, laid end to end along the dimension named above; an argument that names none is the same for every part. Nothing has to cross between parts.
Inputs may be any that keep to these rules, and one draw needn't show every extreme that they name: Within each aligned block of 768 tokens final_order is a permutation of 0 to 767.
All inputs are finite; a program needn't handle non-finite values.
Results may differ from the reference program's by a relative error of at most 0.0058.
Values may be sent and summed in bfloat16 or wider, within the bound.
A program may use at most 192 MiB of HBM per device.

```python
import math
import jax
import jax.numpy as jnp
from jax import lax

D = 8192
TOK_DEV = 768
LAYERS = 2
TOKENS = 1536
N_DP = 2


def draw_final_order(key, part):
    subkeys = jax.random.split(key, TOKENS // TOK_DEV)
    orderings = jax.vmap(lambda single: jax.random.permutation(single, TOK_DEV))(subkeys)
    return orderings.reshape(TOKENS).astype(jnp.int32)


def steps_of(rng, dims, cuts, smallest, largest):
    loudness = 1.0
    for axis_at, parts in cuts:
        draws = jax.random.uniform(jax.random.fold_in(jax.random.fold_in(rng, 6), axis_at), (parts,), jnp.float32, smallest / len(cuts), largest / len(cuts))
        loudness = loudness * jnp.repeat(jnp.exp(draws), dims[axis_at] // parts).reshape((-1,) + (1,) * (len(dims) - 1 - axis_at))
    return loudness


def gaussian(own_key, shape, width, bound, cuts=(), kind=jnp.bfloat16):
    entries = width * jax.random.normal(own_key, shape, jnp.float32)
    if cuts:
        entries = entries * steps_of(own_key, shape, cuts, -0.22, 0.18)
    return jnp.clip(entries, -bound, bound).astype(kind)


def setup_inputs(seed: int = 0, part: int = 0) -> dict:
    key_list = jax.random.split(jax.random.key(seed), 6)
    own_keys = jax.random.split(jax.random.fold_in(key_list[5], part), 6)
    residuals = gaussian(own_keys[0], (LAYERS, TOKENS, D), 1.0, 6.0, ((0, 2), (1, 2), (2, 4)))
    final_resid = gaussian(own_keys[1], (TOKENS, D), 1.0, 6.0, ((0, 4), (1, 4)))
    final_order = draw_final_order(jax.random.fold_in(jax.random.fold_in(key_list[5], part), 71), part)
    translator = gaussian(key_list[3], (LAYERS, D, D), D ** -0.5, 0.0625, ((0, 2), (1, 2), (2, 4)))
    bias = gaussian(key_list[4], (LAYERS, D), 1.0, 5.0, ((0, 2), (1, 4)), jnp.float32)
    return dict(residuals=residuals, final_resid=final_resid, final_order=final_order, translator=translator, bias=bias)


def reference(residuals, final_resid, final_order, translator, bias):
    blocks = final_resid.reshape(N_DP, TOK_DEV, D)
    orders = final_order.reshape(N_DP, TOK_DEV).astype(jnp.int32)
    targets = jax.vmap(lambda block_rows, positions: block_rows[positions])(blocks, orders)
    targets = targets.reshape(TOKENS, D).astype(jnp.float32)
    factor = 1.0 / math.sqrt(TOKENS)
    weight_grads = []
    bias_grads = []
    for layer_index in range(LAYERS):
        inputs = residuals[layer_index]
        predicted = inputs.astype(jnp.float32) + jnp.dot(inputs, translator[layer_index], preferred_element_type=jnp.float32) + bias[layer_index]
        scaled_error = (predicted - targets) * factor
        bias_grads.append(lax.optimization_barrier(jnp.sum(scaled_error, axis=0)))
        rounded = scaled_error.astype(jnp.bfloat16)
        summed = jnp.zeros((D, D), jnp.float32)
        for block_index in range(N_DP):
            first_row = block_index * TOK_DEV
            partial_sum = lax.dot_general(inputs[first_row:first_row + TOK_DEV], rounded[first_row:first_row + TOK_DEV], (((0,), (0,)), ((), ())), preferred_element_type=jnp.float32)
            partial_sum = lax.optimization_barrier(partial_sum.astype(jnp.bfloat16))
            summed = summed + partial_sum.astype(jnp.float32)
        weight_grads.append(summed.astype(jnp.bfloat16))
    return (jnp.stack(weight_grads), jnp.stack(bias_grads))
```

```python
import math

import jax
import jax.numpy as jnp
from jax import lax
from jax.sharding import PartitionSpec as P

CHUNKS = 2


def on_device(residuals, final_resid, final_order, translator, bias):
    own = residuals[0]
    weight = translator[0]
    tokens = own.shape[0]
    ways = lax.axis_size("dp")
    factor = 1.0 / math.sqrt(tokens * ways)
    gathered_final = lax.all_gather(final_resid, "section", axis=0, tiled=True)
    targets = gathered_final[final_order].astype(jnp.float32)
    step = tokens // CHUNKS
    inputs, errors = [], []
    grad_b = 0.0
    for c in range(CHUNKS):
        rows = slice(c * step, (c + 1) * step)
        wide = lax.all_gather(own[rows], "feat", axis=1, tiled=True)
        halves = jnp.stack(jnp.split(wide, ways, axis=1))
        mine = lax.all_to_all(halves, "dp", split_axis=0, concat_axis=0, tiled=True)
        mine = mine.reshape(ways * step, -1)
        part = jnp.dot(mine, weight, preferred_element_type=jnp.float32).astype(jnp.bfloat16)
        parts = lax.all_to_all(
            part.reshape(ways, step, -1), "dp", split_axis=0, concat_axis=0, tiled=True
        )
        product = jnp.sum(parts.astype(jnp.float32), axis=0)
        scaled = (own[rows].astype(jnp.float32) + product + bias[0] - targets[rows]) * factor
        grad_b = grad_b + jnp.sum(scaled, axis=0)
        inputs.append(mine)
        errors.append(lax.all_gather(scaled.astype(jnp.bfloat16), "dp", axis=0, tiled=True))
    grad_b = lax.psum(grad_b, "dp")
    grad_w = lax.dot_general(
        jnp.concatenate(inputs), jnp.concatenate(errors), (((0,), (0,)), ((), ())),
        preferred_element_type=jnp.float32,
    ).astype(jnp.bfloat16)
    return (grad_w[None], grad_b[None])


def solution(mesh):
    placed = (
        P("section", ("groups", "dp"), "feat"),
        P(("groups", "dp", "section"), "feat"),
        P(("groups", "dp")),
        P("section", "dp", "feat"),
        P("section", "feat"),
    )
    return jax.shard_map(
        on_device,
        mesh=mesh,
        in_specs=placed,
        out_specs=(P(("groups", "section"), "dp", "feat"), P(("groups", "section"), "feat")),
        check_vma=False,
    )
```

```python
import functools
import math

import jax
import jax.numpy as jnp
from jax import lax
from jax.experimental import pallas as pl
from jax.experimental.pallas import tpu as pltpu
from jax.sharding import PartitionSpec as P

CHUNKS = 6
MESH = pl.DeviceIdType.MESH


def dot(a, b):
    return jnp.dot(a, b, preferred_element_type=jnp.float32)


def exchange_kernel(
    chunks, factor, own_hbm, fin_hbm, order_ref, w_hbm, bias_ref,
    x_out, e_out, gb_out,
    slabs, transit, own, fin, w, p_send, p_recv, mine, err, gb,
    load_sem, fin_sem, send_sem, recv_sem, p_sem, e_sem, gb_sem, out_sem,
):
    h = lax.axis_index("dp")
    f = lax.axis_index("feat")
    core = lax.axis_index("section")
    way = 1 - 2 * h
    g = f * way + 3 * h
    outer, inner = h, 1 - h
    tokens, width = own.shape
    step = tokens // chunks
    up, down, across = {"feat": f + way}, {"feat": f - way}, {"dp": 1 - h}
    sibling = {"section": 1 - core}
    half = fin_hbm.shape[0]

    def rows(c):
        return pl.ds(pl.multiple_of(c * step, step), step)

    def place(k, c):
        if k == 4:
            return transit.at[rows(c)]
        return slabs.at[(outer, outer, inner, inner)[k], k % 2, rows(c)]

    def landing(k, c):
        return slabs.at[(inner, inner, outer, outer)[k], k % 2, rows(c)]

    def along(src, k, slot, to, c):
        return pltpu.make_async_remote_copy(
            src_ref=src, dst_ref=place(k, c), send_sem=send_sem.at[slot, c],
            recv_sem=recv_sem.at[k, c], device_id=to, device_id_type=MESH)

    def over(src, k, c):
        return pltpu.make_async_remote_copy(
            src_ref=src, dst_ref=landing(k, c), send_sem=send_sem.at[0, c],
            recv_sem=recv_sem.at[k, c], device_id=across, device_id_type=MESH)

    def rise(k, c, src=None):
        return along(place(k, c) if src is None else src, k, 1 + k, up, c)

    def sink(k, c, src=None):
        return along(place(k, c) if src is None else src, k, 3 + k, down, c)

    def arrived(k, c):
        along(place(k, c), k, 0, across, c).wait_recv()

    def at(*positions):
        hit = g == positions[0]
        for p in positions[1:]:
            hit = jnp.logical_or(hit, g == p)
        return pl.when(hit)

    load_own = pltpu.make_async_copy(own_hbm, own, load_sem.at[0])
    load_w = pltpu.make_async_copy(w_hbm, w, load_sem.at[1])
    keep_outer = pltpu.make_async_copy(own_hbm, slabs.at[outer, 0], load_sem.at[2])
    keep_inner = pltpu.make_async_copy(own_hbm, slabs.at[inner, 0], load_sem.at[2])
    fin_rows = fin.at[pl.ds(pl.multiple_of(core * half, half), half)]
    load_fin = pltpu.make_async_copy(fin_hbm, fin_rows, load_sem.at[3])
    load_own.start()
    load_fin.start()
    at(0)(keep_outer.start)
    at(1)(keep_inner.start)
    load_w.start()
    gb[0] = jnp.zeros_like(gb[0])

    barrier = pltpu.get_barrier_semaphore()
    for to in (across, sibling):
        pl.semaphore_signal(barrier, inc=1, device_id=to, device_id_type=MESH)

    @at(0, 1, 2)
    def _():
        pl.semaphore_signal(barrier, inc=1, device_id=up, device_id_type=MESH)

    @at(1, 2, 3)
    def _():
        pl.semaphore_signal(barrier, inc=1, device_id=down, device_id_type=MESH)

    @at(0, 3)
    def _():
        pl.semaphore_wait(barrier, 3)

    @at(1, 2)
    def _():
        pl.semaphore_wait(barrier, 4)

    load_own.wait()
    load_fin.wait()
    send_fin = pltpu.make_async_remote_copy(
        src_ref=fin_rows, dst_ref=fin_rows, send_sem=fin_sem.at[0],
        recv_sem=fin_sem.at[1], device_id=sibling, device_id_type=MESH)
    send_fin.start()

    def start_own(c):
        src = own.at[rows(c)]

        @at(0)
        def _():
            rise(0, c, src).start()

        @at(1)
        def _():
            rise(2, c, src).start()
            sink(2, c, src).start()

        @at(2)
        def _():
            over(src, 3, c).start()

        @at(3)
        def _():
            over(src, 1, c).start()
            sink(4, c, src).start()

    def forward(c):
        @at(0)
        def _():
            arrived(1, c)
            rise(1, c).start()
            arrived(4, c)
            over(place(4, c), 1, c).start()

        @at(1)
        def _():
            arrived(0, c)
            rise(0, c).start()
            arrived(3, c)
            rise(3, c).start()
            sink(3, c).start()
            arrived(4, c)
            over(place(4, c), 1, c).start()
            sink(4, c).start()

        @at(2)
        def _():
            arrived(4, c)
            sink(4, c).start()
            for k in (0, 2, 3):
                arrived(k, c)
                rise(k, c).start()

    def collect(c):
        @at(0)
        def _():
            arrived(2, c)
            arrived(3, c)

        @at(1, 2)
        def _():
            arrived(1, c)

        @at(3)
        def _():
            for k in range(4):
                arrived(k, c)

    def finish(c):
        src = own.at[rows(c)]

        @at(0)
        def _():
            rise(0, c, src).wait_send()
            rise(1, c).wait_send()
            over(place(4, c), 1, c).wait_send()

        @at(1)
        def _():
            rise(2, c, src).wait_send()
            sink(2, c, src).wait_send()
            rise(0, c).wait_send()
            rise(3, c).wait_send()
            sink(3, c).wait_send()
            over(place(4, c), 1, c).wait_send()
            sink(4, c).wait_send()

        @at(2)
        def _():
            over(src, 3, c).wait_send()
            sink(4, c).wait_send()
            for k in (0, 2, 3):
                rise(k, c).wait_send()

        @at(3)
        def _():
            over(src, 1, c).wait_send()
            sink(4, c, src).wait_send()

    def send_p(c):
        return pltpu.make_async_remote_copy(
            src_ref=p_send.at[rows(c)], dst_ref=p_recv.at[rows(c)], send_sem=p_sem.at[0, c],
            recv_sem=p_sem.at[1, c], device_id=across, device_id_type=MESH)

    def send_e(c):
        return pltpu.make_async_remote_copy(
            src_ref=err.at[0, rows(c)], dst_ref=err.at[1, rows(c)], send_sem=e_sem.at[0, c],
            recv_sem=e_sem.at[1, c], device_id=across, device_id_type=MESH)

    def keep_x(c):
        return pltpu.make_async_copy(
            slabs.at[:, :, rows(c)], x_out.at[:, :, rows(c)], out_sem.at[c])

    tile = min(512, width)

    def compute(c):
        collect(c)
        keep_x(c).start()

        @pl.loop(0, width // tile)
        def _(n):
            cols = pl.ds(pl.multiple_of(n * tile, tile), tile)
            other = dot(slabs[0, 1, rows(c)], w[0, :, cols]) + dot(slabs[1, 1, rows(c)], w[1, :, cols])
            p_send[rows(c), cols] = other.astype(p_send.dtype)

        send_p(c).start()
        chosen = order_ref[rows(c)] == lax.broadcasted_iota(jnp.int32, (step, tokens), 1)
        chosen = jnp.where(chosen, 1.0, 0.0).astype(fin.dtype)

        @pl.loop(0, width // tile)
        def _(n):
            cols = pl.ds(pl.multiple_of(n * tile, tile), tile)
            value = dot(slabs[0, 0, rows(c)], w[0, :, cols]) + dot(slabs[1, 0, rows(c)], w[1, :, cols])
            target = dot(chosen, fin[:, cols])
            mine[c % 2, :, cols] = own[rows(c), cols].astype(jnp.float32) + value + bias_ref[:, cols] - target

    def settle(c):
        send_p(c).wait_recv()

        @pl.loop(0, width // tile)
        def _(n):
            cols = pl.ds(pl.multiple_of(n * tile, tile), tile)
            scaled = (mine[c % 2, :, cols] + p_recv[rows(c), cols].astype(jnp.float32)) * factor
            err[0, rows(c), cols] = scaled.astype(err.dtype)
            gb[0, :, cols] += jnp.sum(scaled.reshape(step // 8, 8, tile), axis=0)

        send_e(c).start()

    start_own(0)
    start_own(1)

    @pl.loop(0, chunks + 2)
    def _(s):
        @pl.when(s + 2 < chunks)
        def _():
            start_own(s + 2)

        @pl.when(s < chunks)
        def _():
            forward(s)

        @pl.when(s == 1)
        def _():
            at(0)(keep_outer.wait)
            at(1)(keep_inner.wait)
            load_w.wait()
            send_fin.wait()

        @pl.when(jnp.logical_and(s >= 1, s <= chunks))
        def _():
            compute(s - 1)

        @pl.when(s >= 2)
        def _():
            settle(s - 2)

    send_gb = pltpu.make_async_remote_copy(
        src_ref=gb.at[0], dst_ref=gb.at[1], send_sem=gb_sem.at[0], recv_sem=gb_sem.at[1],
        device_id=across, device_id_type=MESH)
    send_gb.start()

    @pl.loop(0, chunks)
    def _(c):
        finish(c)
        send_p(c).wait_send()
        send_e(c).wait()
        keep_x(c).wait()

    send_gb.wait()
    keep_e = pltpu.make_async_copy(err, e_out, load_sem.at[0])
    keep_e.start()
    gb_out[...] = jnp.sum(gb[0] + gb[1], axis=0, keepdims=True)
    keep_e.wait()


def paired(residuals, final_resid, final_order, translator, bias):
    own = residuals[0]
    tokens, width = own.shape
    factor = 1.0 / math.sqrt(tokens * lax.axis_size("dp"))
    weight = translator[0].reshape(2, width, -1)
    bf16, f32 = own.dtype, jnp.float32
    hbm = pl.BlockSpec(memory_space=pl.ANY)
    vmem = pl.BlockSpec(memory_space=pltpu.VMEM)
    dma = pltpu.SemaphoreType.DMA
    x_all, e_all, grad_b = pl.pallas_call(
        functools.partial(exchange_kernel, CHUNKS, factor),
        out_shape=(
            jax.ShapeDtypeStruct((2, 2, tokens, width), bf16),
            jax.ShapeDtypeStruct((2, tokens, width), bf16),
            jax.ShapeDtypeStruct((1, width), f32),
        ),
        in_specs=[hbm, hbm, vmem, hbm, vmem],
        out_specs=(hbm, hbm, vmem),
        scratch_shapes=[
            pltpu.VMEM((2, 2, tokens, width), bf16),
            pltpu.VMEM((tokens, width), bf16),
            pltpu.VMEM((tokens, width), bf16),
            pltpu.VMEM((tokens, width), bf16),
            pltpu.VMEM(weight.shape, bf16),
            pltpu.VMEM((tokens, width), bf16),
            pltpu.VMEM((tokens, width), bf16),
            pltpu.VMEM((2, tokens // CHUNKS, width), f32),
            pltpu.VMEM((2, tokens, width), bf16),
            pltpu.VMEM((2, 8, width), f32),
            dma((4,)),
            dma((2,)),
            dma((8, CHUNKS)),
            dma((5, CHUNKS)),
            dma((2, CHUNKS)),
            dma((2, CHUNKS)),
            dma((2,)),
            dma((CHUNKS,)),
        ],
        compiler_params=pltpu.CompilerParams(
            collective_id=0, has_side_effects=True, vmem_limit_bytes=60 * 1024 * 1024),
        name="exchange",
    )(own, final_resid, final_order[:, None], weight, bias)
    x_all = x_all.reshape(2, 2 * tokens, width)
    e_all = e_all.reshape(2 * tokens, width)
    grad_w = lax.dot_general(
        x_all, e_all, (((1,), (0,)), ((), ())), preferred_element_type=f32
    ).astype(bf16)
    return grad_w.reshape(1, 2 * width, -1), grad_b


def general(residuals, final_resid, final_order, translator, bias):
    own = residuals[0]
    weight = translator[0]
    tokens = own.shape[0]
    ways = lax.axis_size("dp")
    factor = 1.0 / math.sqrt(tokens * ways)
    gathered_final = lax.all_gather(final_resid, "section", axis=0, tiled=True)
    targets = gathered_final[final_order].astype(jnp.float32)
    chunks = 2
    step = tokens // chunks
    inputs, errors = [], []
    grad_b = 0.0
    for c in range(chunks):
        rows = slice(c * step, (c + 1) * step)
        wide = lax.all_gather(own[rows], "feat", axis=1, tiled=True)
        halves = jnp.stack(jnp.split(wide, ways, axis=1))
        mine = lax.all_to_all(halves, "dp", split_axis=0, concat_axis=0, tiled=True)
        mine = mine.reshape(ways * step, -1)
        part = dot(mine, weight).astype(jnp.bfloat16)
        parts = lax.all_to_all(
            part.reshape(ways, step, -1), "dp", split_axis=0, concat_axis=0, tiled=True
        )
        product = jnp.sum(parts.astype(jnp.float32), axis=0)
        scaled = (own[rows].astype(jnp.float32) + product + bias[0] - targets[rows]) * factor
        grad_b = grad_b + jnp.sum(scaled, axis=0)
        inputs.append(mine)
        errors.append(lax.all_gather(scaled.astype(jnp.bfloat16), "dp", axis=0, tiled=True))
    grad_b = lax.psum(grad_b, "dp")
    grad_w = lax.dot_general(
        jnp.concatenate(inputs), jnp.concatenate(errors), (((0,), (0,)), ((), ())),
        preferred_element_type=jnp.float32,
    ).astype(jnp.bfloat16)
    return (grad_w[None], grad_b[None])


def solution(mesh):
    placed = (
        P("section", ("groups", "dp"), "feat"),
        P(("groups", "dp", "section"), "feat"),
        P(("groups", "dp")),
        P("section", "dp", "feat"),
        P("section", "feat"),
    )
    sizes = mesh.shape
    fits = sizes["dp"] == 2 and sizes["feat"] == 4 and sizes["section"] == 2
    return jax.shard_map(
        paired if fits else general,
        mesh=mesh,
        in_specs=placed,
        out_specs=(P(("groups", "section"), "dp", "feat"), P(("groups", "section"), "feat")),
        check_vma=False,
    )
```

```python
import functools
import math

import jax
import jax.numpy as jnp
from jax import lax
from jax.experimental import pallas as pl
from jax.experimental.pallas import tpu as pltpu
from jax.sharding import PartitionSpec as P

CHUNKS = 12
EARLY = 8
MESH = pl.DeviceIdType.MESH


def dot(a, b):
    return jnp.dot(a, b, preferred_element_type=jnp.float32)


def exchange_kernel(
    chunks, early, factor, own_hbm, fin_hbm, order_ref, w_hbm, bias_ref,
    x_out, e_out, gb_out, part_out,
    slabs, transit, own, fin, w, p_send, p_recv, mine, err, gb, stage,
    load_sem, fin_sem, send_sem, recv_sem, p_sem, e_sem, gb_sem, out_sem, part_sem,
):
    h = lax.axis_index("dp")
    f = lax.axis_index("feat")
    core = lax.axis_index("section")
    way = 1 - 2 * h
    g = f * way + 3 * h
    outer, inner = h, 1 - h
    tokens, width = own.shape
    step = tokens // chunks
    up, down, across = {"feat": f + way}, {"feat": f - way}, {"dp": 1 - h}
    sibling = {"section": 1 - core}
    half = fin_hbm.shape[0]

    def rows(c):
        return pl.ds(pl.multiple_of(c * step, step), step)

    def place(k, c):
        if k == 4:
            return transit.at[rows(c)]
        return slabs.at[(outer, outer, inner, inner)[k], k % 2, rows(c)]

    def landing(k, c):
        return slabs.at[(inner, inner, outer, outer)[k], k % 2, rows(c)]

    def along(src, k, slot, to, c):
        return pltpu.make_async_remote_copy(
            src_ref=src, dst_ref=place(k, c), send_sem=send_sem.at[slot, c],
            recv_sem=recv_sem.at[k, c], device_id=to, device_id_type=MESH)

    def over(src, k, c):
        return pltpu.make_async_remote_copy(
            src_ref=src, dst_ref=landing(k, c), send_sem=send_sem.at[0, c],
            recv_sem=recv_sem.at[k, c], device_id=across, device_id_type=MESH)

    def rise(k, c, src=None):
        return along(place(k, c) if src is None else src, k, 1 + k, up, c)

    def sink(k, c, src=None):
        return along(place(k, c) if src is None else src, k, 3 + k, down, c)

    def arrived(k, c):
        along(place(k, c), k, 0, across, c).wait_recv()

    def at(*positions):
        hit = g == positions[0]
        for p in positions[1:]:
            hit = jnp.logical_or(hit, g == p)
        return pl.when(hit)

    load_own = pltpu.make_async_copy(own_hbm, own, load_sem.at[0])
    load_w = pltpu.make_async_copy(w_hbm, w, load_sem.at[1])
    keep_outer = pltpu.make_async_copy(own_hbm, slabs.at[outer, 0], load_sem.at[2])
    keep_inner = pltpu.make_async_copy(own_hbm, slabs.at[inner, 0], load_sem.at[2])
    fin_rows = fin.at[pl.ds(pl.multiple_of(core * half, half), half)]
    load_fin = pltpu.make_async_copy(fin_hbm, fin_rows, load_sem.at[3])
    load_own.start()
    load_fin.start()
    at(0)(keep_outer.start)
    at(1)(keep_inner.start)
    load_w.start()
    gb[0] = jnp.zeros_like(gb[0])

    barrier = pltpu.get_barrier_semaphore()
    for to in (across, sibling):
        pl.semaphore_signal(barrier, inc=1, device_id=to, device_id_type=MESH)

    @at(0, 1, 2)
    def _():
        pl.semaphore_signal(barrier, inc=1, device_id=up, device_id_type=MESH)

    @at(1, 2, 3)
    def _():
        pl.semaphore_signal(barrier, inc=1, device_id=down, device_id_type=MESH)

    @at(0, 3)
    def _():
        pl.semaphore_wait(barrier, 3)

    @at(1, 2)
    def _():
        pl.semaphore_wait(barrier, 4)

    load_own.wait()
    load_fin.wait()
    send_fin = pltpu.make_async_remote_copy(
        src_ref=fin_rows, dst_ref=fin_rows, send_sem=fin_sem.at[0],
        recv_sem=fin_sem.at[1], device_id=sibling, device_id_type=MESH)
    send_fin.start()

    def start_own(c):
        src = own.at[rows(c)]

        @at(0)
        def _():
            rise(0, c, src).start()

        @at(1)
        def _():
            rise(2, c, src).start()
            sink(2, c, src).start()

        @at(2)
        def _():
            over(src, 3, c).start()

        @at(3)
        def _():
            over(src, 1, c).start()
            sink(4, c, src).start()

    def forward(c):
        @at(0)
        def _():
            arrived(1, c)
            rise(1, c).start()
            arrived(4, c)
            over(place(4, c), 1, c).start()

        @at(1)
        def _():
            arrived(0, c)
            rise(0, c).start()
            arrived(3, c)
            rise(3, c).start()
            sink(3, c).start()
            arrived(4, c)
            over(place(4, c), 1, c).start()
            sink(4, c).start()

        @at(2)
        def _():
            arrived(4, c)
            sink(4, c).start()
            for k in (0, 2, 3):
                arrived(k, c)
                rise(k, c).start()

    def collect(c):
        @at(0)
        def _():
            arrived(2, c)
            arrived(3, c)

        @at(1, 2)
        def _():
            arrived(1, c)

        @at(3)
        def _():
            for k in range(4):
                arrived(k, c)

    def finish(c):
        src = own.at[rows(c)]

        @at(0)
        def _():
            rise(0, c, src).wait_send()
            rise(1, c).wait_send()
            over(place(4, c), 1, c).wait_send()

        @at(1)
        def _():
            rise(2, c, src).wait_send()
            sink(2, c, src).wait_send()
            rise(0, c).wait_send()
            rise(3, c).wait_send()
            sink(3, c).wait_send()
            over(place(4, c), 1, c).wait_send()
            sink(4, c).wait_send()

        @at(2)
        def _():
            over(src, 3, c).wait_send()
            sink(4, c).wait_send()
            for k in (0, 2, 3):
                rise(k, c).wait_send()

        @at(3)
        def _():
            over(src, 1, c).wait_send()
            sink(4, c, src).wait_send()

    def send_p(c):
        return pltpu.make_async_remote_copy(
            src_ref=p_send.at[rows(c)], dst_ref=p_recv.at[rows(c)], send_sem=p_sem.at[0, c],
            recv_sem=p_sem.at[1, c], device_id=across, device_id_type=MESH)

    def send_e(c):
        return pltpu.make_async_remote_copy(
            src_ref=err.at[0, rows(c)], dst_ref=err.at[1, rows(c)], send_sem=e_sem.at[0, c],
            recv_sem=e_sem.at[1, c], device_id=across, device_id_type=MESH)

    def keep_x(c):
        return pltpu.make_async_copy(
            slabs.at[:, :, rows(c)], x_out.at[:, :, rows(c - early)], out_sem.at[c])

    tile = min(512, width)

    def compute(c):
        collect(c)
        pl.when(c >= early)(keep_x(c).start)

        chosen = order_ref[rows(c)] == lax.broadcasted_iota(jnp.int32, (step, tokens), 1)
        chosen = jnp.where(chosen, 1.0, 0.0).astype(fin.dtype)

        @pl.loop(0, width // tile)
        def _(n):
            cols = pl.ds(pl.multiple_of(n * tile, tile), tile)
            value = sum(dot(slabs[i, :, rows(c)].reshape(2 * step, width), w[i, :, cols]) for i in range(2))
            p_send[rows(c), cols] = value[step:].astype(p_send.dtype)
            target = dot(chosen, fin[:, cols])
            mine[c % 2, :, cols] = own[rows(c), cols].astype(jnp.float32) + value[:step] + bias_ref[:, cols] - target

        send_p(c).start()

    def settle(c):
        send_p(c).wait_recv()

        @pl.loop(0, width // tile)
        def _(n):
            cols = pl.ds(pl.multiple_of(n * tile, tile), tile)
            scaled = (mine[c % 2, :, cols] + p_recv[rows(c), cols].astype(jnp.float32)) * factor
            err[0, rows(c), cols] = scaled.astype(err.dtype)
            gb[0, :, cols] += jnp.sum(scaled.reshape(step // 8, 8, tile), axis=0)

        send_e(c).start()

    ready = early * step
    band = stage.shape[1]
    bands = width // band
    breadth = min(1024, width)

    def keep_part(i, q):
        j = 2 * i + q
        first = pl.multiple_of((j % bands) * band, band)
        return pltpu.make_async_copy(
            stage.at[q], part_out.at[j // bands, pl.ds(first, band)], part_sem.at[q])

    def early_gradient(i):
        for q in range(2):
            j = 2 * i + q
            pl.when(i > 0)(keep_part(i, q).wait)
            first = pl.multiple_of((j % bands) * band, band)
            left = slabs[j // bands, :, :ready, pl.ds(first, band)].reshape(2 * ready, band)

            @pl.loop(0, width // breadth)
            def _(n):
                cols = pl.ds(pl.multiple_of(n * breadth, breadth), breadth)
                right = err[:, :ready, cols].reshape(2 * ready, breadth)
                value = lax.dot_general(
                    left, right, (((0,), (0,)), ((), ())), preferred_element_type=jnp.float32)
                stage[q, :, cols] = value.astype(stage.dtype)

            keep_part(i, q).start()

    start_own(0)
    start_own(1)

    @pl.loop(0, chunks + 2)
    def _(s):
        @pl.when(s + 2 < chunks)
        def _():
            start_own(s + 2)

        @pl.when(s < chunks)
        def _():
            forward(s)

        @pl.when(s == 1)
        def _():
            at(0)(keep_outer.wait)
            at(1)(keep_inner.wait)
            load_w.wait()
            send_fin.wait()

        @pl.when(jnp.logical_and(s >= 1, s <= chunks))
        def _():
            compute(s - 1)

        @pl.when(s == early + 2)
        def _():
            @pl.loop(0, early)
            def _(c):
                send_e(c).wait_recv()

        @pl.when(jnp.logical_and(s >= early + 2, s < early + 2 + bands))
        def _():
            early_gradient(s - early - 2)

        @pl.when(s >= 2)
        def _():
            settle(s - 2)

    send_gb = pltpu.make_async_remote_copy(
        src_ref=gb.at[0], dst_ref=gb.at[1], send_sem=gb_sem.at[0], recv_sem=gb_sem.at[1],
        device_id=across, device_id_type=MESH)
    send_gb.start()

    @pl.loop(0, chunks)
    def _(c):
        finish(c)
        send_p(c).wait_send()
        send_e(c).wait_send()

        @pl.when(c >= early)
        def _():
            send_e(c).wait_recv()
            keep_x(c).wait()

    send_gb.wait()
    for q in range(2):
        keep_part(bands - 1, q).wait()
    keep_e = pltpu.make_async_copy(err.at[:, ready:], e_out, load_sem.at[0])
    keep_e.start()
    gb_out[...] = jnp.sum(gb[0] + gb[1], axis=0, keepdims=True)
    keep_e.wait()


def paired(residuals, final_resid, final_order, translator, bias):
    own = residuals[0]
    tokens, width = own.shape
    factor = 1.0 / math.sqrt(tokens * lax.axis_size("dp"))
    weight = translator[0].reshape(2, width, -1)
    late = tokens - EARLY * (tokens // CHUNKS)
    bf16, f32 = own.dtype, jnp.float32
    hbm = pl.BlockSpec(memory_space=pl.ANY)
    vmem = pl.BlockSpec(memory_space=pltpu.VMEM)
    dma = pltpu.SemaphoreType.DMA
    x_all, e_all, grad_b, part = pl.pallas_call(
        functools.partial(exchange_kernel, CHUNKS, EARLY, factor),
        out_shape=(
            jax.ShapeDtypeStruct((2, 2, late, width), bf16),
            jax.ShapeDtypeStruct((2, late, width), bf16),
            jax.ShapeDtypeStruct((1, width), f32),
            jax.ShapeDtypeStruct((2, width, width), bf16),
        ),
        in_specs=[hbm, hbm, vmem, hbm, vmem],
        out_specs=(hbm, hbm, vmem, hbm),
        scratch_shapes=[
            pltpu.VMEM((2, 2, tokens, width), bf16),
            pltpu.VMEM((tokens, width), bf16),
            pltpu.VMEM((tokens, width), bf16),
            pltpu.VMEM((tokens, width), bf16),
            pltpu.VMEM(weight.shape, bf16),
            pltpu.VMEM((tokens, width), bf16),
            pltpu.VMEM((tokens, width), bf16),
            pltpu.VMEM((2, tokens // CHUNKS, width), f32),
            pltpu.VMEM((2, tokens, width), bf16),
            pltpu.VMEM((2, 8, width), f32),
            pltpu.VMEM((2, width // 4, width), bf16),
            dma((4,)),
            dma((2,)),
            dma((8, CHUNKS)),
            dma((5, CHUNKS)),
            dma((2, CHUNKS)),
            dma((2, CHUNKS)),
            dma((2,)),
            dma((CHUNKS,)),
            dma((2,)),
        ],
        compiler_params=pltpu.CompilerParams(
            collective_id=0, has_side_effects=True, vmem_limit_bytes=60 * 1024 * 1024),
        name="exchange",
    )(own, final_resid, final_order[:, None], weight, bias)
    x_all = x_all.reshape(2, 2 * late, width)
    e_all = e_all.reshape(2 * late, width)
    grad_w = lax.dot_general(
        x_all, e_all, (((1,), (0,)), ((), ())), preferred_element_type=f32
    )
    grad_w = (grad_w + part.astype(f32)).astype(bf16)
    return grad_w.reshape(1, 2 * width, -1), grad_b


def general(residuals, final_resid, final_order, translator, bias):
    own = residuals[0]
    weight = translator[0]
    tokens = own.shape[0]
    ways = lax.axis_size("dp")
    factor = 1.0 / math.sqrt(tokens * ways)
    gathered_final = lax.all_gather(final_resid, "section", axis=0, tiled=True)
    targets = gathered_final[final_order].astype(jnp.float32)
    chunks = 2
    step = tokens // chunks
    inputs, errors = [], []
    grad_b = 0.0
    for c in range(chunks):
        rows = slice(c * step, (c + 1) * step)
        wide = lax.all_gather(own[rows], "feat", axis=1, tiled=True)
        halves = jnp.stack(jnp.split(wide, ways, axis=1))
        mine = lax.all_to_all(halves, "dp", split_axis=0, concat_axis=0, tiled=True)
        mine = mine.reshape(ways * step, -1)
        part = dot(mine, weight).astype(jnp.bfloat16)
        parts = lax.all_to_all(
            part.reshape(ways, step, -1), "dp", split_axis=0, concat_axis=0, tiled=True
        )
        product = jnp.sum(parts.astype(jnp.float32), axis=0)
        scaled = (own[rows].astype(jnp.float32) + product + bias[0] - targets[rows]) * factor
        grad_b = grad_b + jnp.sum(scaled, axis=0)
        inputs.append(mine)
        errors.append(lax.all_gather(scaled.astype(jnp.bfloat16), "dp", axis=0, tiled=True))
    grad_b = lax.psum(grad_b, "dp")
    grad_w = lax.dot_general(
        jnp.concatenate(inputs), jnp.concatenate(errors), (((0,), (0,)), ((), ())),
        preferred_element_type=jnp.float32,
    ).astype(jnp.bfloat16)
    return (grad_w[None], grad_b[None])


def solution(mesh):
    placed = (
        P("section", ("groups", "dp"), "feat"),
        P(("groups", "dp", "section"), "feat"),
        P(("groups", "dp")),
        P("section", "dp", "feat"),
        P("section", "feat"),
    )
    sizes = mesh.shape
    fits = sizes["dp"] == 2 and sizes["feat"] == 4 and sizes["section"] == 2
    return jax.shard_map(
        paired if fits else general,
        mesh=mesh,
        in_specs=placed,
        out_specs=(P(("groups", "section"), "dp", "feat"), P(("groups", "section"), "feat")),
        check_vma=False,
    )
```
